32 devices in a mesh: pole: 4 (over z), row: 2 (over x), col: 4 (over y, core).
Axes of the slice: x: 2, y: 2, z: 4, core: 2. Of those that a mesh axis runs over, the one named last changes fastest.
Arguments:
- trailing: float32 [4, 2, 4096, 4096], P('pole', None, 'col', 'row'), may hold values from -6 to 6
- lower_panel: float32 [4, 3, 2, 512, 4096], P('pole', None, None, 'col', 'row'), may hold values from -0.09375 to 0.09375
- pivot_inverse: float32 [4, 3, 2, 512, 512], P('pole', None, None, 'col', 'row'), may hold values from -6 to 6
- pole_weights: float32 [4, 2], P('pole'), may hold values from -3 to 3
- listed: int32 [3, 8], replicated, may hold values from 0 to 15, as said below
- list_counts: int32 [3], replicated, may hold values from 1 to 8, as said below
Outputs:
- off_inverse: float32 [4, 3, 2, 512, 4096], P('pole', None, None, 'row', 'col')
- density: float32 [3, 2, 512, 512], P(None, None, 'col', 'row')
The draws below stay inside these ranges and needn't reach their ends.
Inputs may be any that keep to these rules, and one draw needn't show every extreme that they name: `listed`: each row holds 8 distinct block numbers in increasing order; only the first list_counts entries are used. `list_counts`: some supernode uses all 8 slots and some other supernode uses fewer.
All inputs are finite; a program needn't handle non-finite values.
Results may differ from the reference program's by a relative error of at most 0.0001.
Values sent between devices are 32-bit elements; how exact they have to be, the bound alone decides.
No kernel may reach another device: no remote copies, remote signals or barrier semaphores. Data moves between devices by JAX's collectives and lax.ppermute only.
A program may use at most 192 MiB of HBM per device.

```python
import jax
import jax.numpy as jnp
from jax import lax

N = 4096
W = 512
BLK = 256
NBLK = 16
LMAX = 8
SUPER = 3
POLES = 4


def draw_listed(key, part):
    keys = jax.random.split(jax.random.fold_in(key, 11), SUPER)
    orders = jax.vmap(lambda one_key: jax.random.permutation(one_key, NBLK))(keys)
    return jnp.sort(orders[:, :LMAX], axis=1).astype(jnp.int32)


def draw_list_counts(key, part):
    counts = jax.random.randint(jax.random.fold_in(key, 21), (SUPER,), 1, LMAX)
    fullest = jax.random.randint(jax.random.fold_in(key, 22), (), 0, SUPER)
    return jnp.where(jnp.arange(SUPER) == fullest, LMAX, counts).astype(jnp.int32)


def steps_of(own_key, dims, shards, smallest, largest):
    level, own = 1.0, jax.random.fold_in(own_key, 6)
    for axis_at, shards_of in shards:
        steps = jnp.exp(jax.random.uniform(jax.random.fold_in(own, axis_at), (shards_of,), jnp.float32, smallest / len(shards), largest / len(shards)))
        level = level * jnp.repeat(steps, dims[axis_at] // shards_of).reshape([-1 if axis == axis_at else 1 for axis in range(len(dims))])
    return level


def scatter_about(stream_key, extent, deviation, most, cuts=(), held_as=jnp.bfloat16):
    array = deviation * jax.random.normal(stream_key, extent, jnp.float32)
    if cuts:
        array = array * steps_of(stream_key, extent, cuts, -0.22, 0.18)
    return jnp.clip(array, -most, most).astype(held_as)


def setup_inputs(seed: int = 0) -> dict:
    streams_of = jax.random.split(jax.random.key(seed), 7)
    trailing = scatter_about(streams_of[0], (POLES, 2, N, N), 1.0, 6.0, ((0, 4), (2, 4), (3, 2)), jnp.float32)
    lower_panel = scatter_about(streams_of[1], (POLES, SUPER, 2, W, N), (2 * LMAX * BLK) ** -0.5, 0.09375, ((0, 4), (3, 4), (4, 2)), jnp.float32)
    pivot_inverse = scatter_about(streams_of[2], (POLES, SUPER, 2, W, W), 1.0, 6.0, ((0, 4), (3, 4), (4, 2)), jnp.float32)
    pole_weights = scatter_about(streams_of[3], (POLES, 2), 1.0, 3.0, ((0, 4),), jnp.float32)
    listed = draw_listed(jax.random.fold_in(streams_of[6], 71), 0)
    list_counts = draw_list_counts(jax.random.fold_in(streams_of[6], 71), 0)
    return dict(trailing=trailing, lower_panel=lower_panel, pivot_inverse=pivot_inverse, pole_weights=pole_weights, listed=listed, list_counts=list_counts)


highest = lax.Precision.HIGHEST


def contract(first_op, second_op):
    return lax.dot_general(first_op, second_op, (((1,), (1,)), ((), ())), precision=highest, preferred_element_type=jnp.float32)


def times_transposed(left_re, left_im, right_re, right_im):
    real_part = contract(left_re, right_re) - contract(left_im, right_im)
    imag_part = contract(left_re, right_im) + contract(left_im, right_re)
    return jnp.stack([real_part, imag_part])


def row_flags(listed, list_counts, supernode):
    slots = jnp.arange(LMAX) < list_counts[supernode]
    hits = (listed[supernode][None, :] == jnp.arange(NBLK)[:, None]) & slots[None, :]
    flags = jnp.any(hits, axis=1).astype(jnp.float32)
    return jnp.repeat(flags, BLK)


def reference(trailing, lower_panel, pivot_inverse, pole_weights, listed, list_counts):
    off_all = []
    density = [jnp.zeros((2, W, W), jnp.float32) for supernode in range(SUPER)]
    for pole_index in range(POLES):
        matrix = trailing[pole_index]
        off_pole = []
        for supernode in range(SUPER):
            rowmask = row_flags(listed, list_counts, supernode)
            lmask = lower_panel[pole_index, supernode] * rowmask[None, None, :]
            offblock = -times_transposed(lmask[0], lmask[1], matrix[0], matrix[1]) * rowmask[None, None, :]
            off_pole.append(offblock)
            corner = pivot_inverse[pole_index, supernode] - times_transposed(lmask[0], lmask[1], offblock[0], offblock[1])
            weight_re = pole_weights[pole_index, 0]
            weight_im = pole_weights[pole_index, 1]
            term = jnp.stack([weight_re * corner[0] - weight_im * corner[1], weight_re * corner[1] + weight_im * corner[0]])
            density[supernode] = density[supernode] + term
        off_all.append(jnp.stack(off_pole))
    return jnp.stack(off_all), jnp.stack(density)
```

```python
import functools
import math

import jax
import jax.numpy as jnp
from jax import lax
from jax.experimental import pallas as pl
from jax.experimental.pallas import tpu as pltpu
from jax.sharding import PartitionSpec as P

BLK = 256
CHUNKS = 2
COL_FRACTIONS = (9 / 24, 11 / 24, 13 / 24, 16 / 24, 1.0)
ROW_FRACTIONS = (5 / 12, 6 / 12, 7 / 12, 9 / 12, 1.0)


def swap(block, axis, bit):
    size = lax.axis_size(axis)
    return lax.ppermute(block, axis, [(at, at ^ bit) for at in range(size)])


def bits_down(size):
    bit = size // 2
    while bit:
        yield bit
        bit //= 2


def gather_xor(block, axis):
    held = {0: block}
    for bit in bits_down(lax.axis_size(axis)):
        held.update({d | bit: swap(b, axis, bit) for d, b in list(held.items())})
    return [held[d] for d in range(len(held))]


def split_terms(value):
    high = value.astype(jnp.bfloat16)
    low = (value - high.astype(jnp.float32)).astype(jnp.bfloat16)
    return high, low


def contract(first_op, second_op):
    return lax.dot_general(
        first_op, second_op, (((1,), (1,)), ((), ())), preferred_element_type=jnp.float32
    )


def left_terms(value):
    high, low = split_terms(value)
    return jnp.concatenate([high, low, high], axis=1)


def right_terms(value):
    high, low = split_terms(value)
    return jnp.concatenate([high, high, low], axis=1)


def quotient(value, by):
    return lax.div(value, jnp.int32(by))


def remainder(value, by):
    return lax.rem(value, jnp.int32(by))


class Plan:
    def __init__(self, supers, slots, blocks, col_blocks, row_blocks):
        self.supers, self.slots, self.blocks = supers, slots, blocks
        self.col_blocks, self.row_blocks = col_blocks, row_blocks
        pairs = supers * slots
        self.pairs = pairs
        self.max_cols = supers * min(col_blocks, slots)
        self.max_rows = supers * min(row_blocks, slots)
        at = 0
        for name, length in (
            ("col_code", self.max_cols),
            ("row_code", self.max_rows),
            ("first_row", supers),
            ("count_row", supers),
            ("part_of_col", pairs),
            ("rank_of_col", pairs),
            ("part_of_row", pairs),
            ("rank_of_row", pairs),
            ("out_slot", supers * row_blocks),
            ("here", 2),
        ):
            setattr(self, name, at)
            at += length
        self.length = at

    def own_col(self, code):
        return remainder(remainder(code, self.blocks), self.col_blocks)

    def own_row(self, code):
        return remainder(remainder(code, self.blocks), self.row_blocks)

    def table(self, listed, list_counts, row, col, row_parts, col_parts):
        pairs = self.pairs
        block = listed.reshape(-1)
        super_of = jnp.arange(pairs) // self.slots
        valid = (jnp.arange(self.slots)[None, :] < list_counts[:, None]).reshape(-1)
        part_col = jnp.where(valid, quotient(block, self.col_blocks), -1)
        part_row = jnp.where(valid, quotient(block, self.row_blocks), -1)
        earlier = jnp.arange(pairs)[None, :] < jnp.arange(pairs)[:, None]

        def ranks(part):
            return jnp.sum((part[None, :] == part[:, None]) & earlier, axis=1)

        rank_col, rank_row = ranks(part_col), ranks(part_row)
        code = super_of * self.blocks + block
        here_col, here_row = part_col == row, part_row == col

        def slots_of(here, rank, value, length, empty):
            hit = here[None, :] & (rank[None, :] == jnp.arange(length)[:, None])
            return jnp.sum(jnp.where(hit, value[None, :] - empty, 0), axis=1) + empty

        col_code = slots_of(here_col, rank_col, code, self.max_cols, -1)
        row_code = slots_of(here_row, rank_row, code, self.max_rows, -1)
        each = jnp.arange(self.supers)[:, None]
        count_row = jnp.sum((super_of[None, :] == each) & here_row[None, :], axis=1)
        first_row = jnp.sum((super_of[None, :] < each) & here_row[None, :], axis=1)
        cell = jnp.arange(self.supers * self.row_blocks)
        cell_code = (
            cell // self.row_blocks * self.blocks + col * self.row_blocks + cell % self.row_blocks
        )
        cell_hit = (code[None, :] == cell_code[:, None]) & valid[None, :]
        out_slot = jnp.sum(jnp.where(cell_hit, rank_row[None, :] + 1, 0), axis=1) - 1
        table = jnp.concatenate(
            [
                col_code,
                row_code,
                first_row,
                count_row,
                part_col,
                rank_col,
                part_row,
                rank_row,
                out_slot,
                jnp.stack([row, col]),
            ]
        ).astype(jnp.int32)
        fill_col = jnp.max(
            jnp.sum(part_col[None, :] == jnp.arange(row_parts)[:, None], axis=1)
        )
        fill_row = jnp.max(
            jnp.sum(part_row[None, :] == jnp.arange(col_parts)[:, None], axis=1)
        )
        return table, fill_col, fill_row


def pack_columns(plan, table, lower_panel, cap, chunks):
    _, _, parts, rows, _ = lower_panel.shape
    chunk = rows // chunks

    def kernel(table_ref, panel_ref, *out_refs):
        for g, out_ref in enumerate(out_refs):
            out_ref[0] = panel_ref[0, 0, :, g * chunk : (g + 1) * chunk, :]

    def panel_at(t, table_ref):
        code = jnp.maximum(table_ref[plan.col_code + t], 0)
        return (0, quotient(code, plan.blocks), 0, 0, plan.own_col(code))

    return pl.pallas_call(
        kernel,
        grid_spec=pltpu.PrefetchScalarGridSpec(
            num_scalar_prefetch=1,
            grid=(cap,),
            in_specs=[pl.BlockSpec((1, 1, parts, rows, BLK), panel_at)],
            out_specs=[
                pl.BlockSpec((1, parts, chunk, BLK), lambda t, table_ref: (t, 0, 0, 0))
                for _ in range(chunks)
            ],
        ),
        out_shape=[
            jax.ShapeDtypeStruct((cap, parts, chunk, BLK), jnp.float32) for _ in range(chunks)
        ],
        name="pack",
    )(table, lower_panel)


def partial_off(plan, table, trailing, gathered, row_cap, row_parts):
    members = len(gathered)
    piece = gathered[0].shape[2]
    share = members // row_parts
    part_rows = share * piece
    rows = members * piece

    def kernel(table_ref, *refs):
        piece_refs = refs[:members]
        trailing_ref = refs[members]
        out_refs = refs[members + 1 : members + 1 + row_parts]
        left_ref = refs[-1]
        t = pl.program_id(0)
        row = table_ref[plan.here]
        col = table_ref[plan.here + 1]
        code = table_ref[plan.col_code + t]
        k = quotient(jnp.maximum(code, 0), plan.blocks)
        first_m = table_ref[plan.first_row + k]
        count = jnp.where(code >= 0, table_ref[plan.count_row + k], 0)

        @pl.when(t == 0)
        def _():
            for out_ref in out_refs:
                out_ref[...] = jnp.zeros(out_ref.shape, jnp.float32)

        @pl.when(count > 0)
        def _():
            for d in range(members):
                member = jnp.bitwise_xor(col, d)
                slot = jnp.bitwise_xor(quotient(member, share), row) * share + remainder(
                    member, share
                )
                at = pl.multiple_of(slot * piece, piece)
                left_re = piece_refs[d][0, 0]
                left_im = piece_refs[d][0, 1]
                left_ref[0, pl.ds(at, piece), :] = left_terms(left_re)
                left_ref[1, pl.ds(at, piece), :] = left_terms(left_im)
                left_ref[2, pl.ds(at, piece), :] = left_terms(left_re + left_im)

        def row_block(m, carry):
            at = pl.multiple_of(plan.own_row(table_ref[plan.row_code + m]) * BLK, BLK)
            right_re = trailing_ref[0, 0, pl.ds(at, BLK), :]
            right_im = trailing_ref[0, 1, pl.ds(at, BLK), :]
            first = contract(left_ref[0], right_terms(right_re))
            second = contract(left_ref[1], right_terms(right_im))
            third = contract(left_ref[2], right_terms(right_re + right_im))
            real = second - first
            imag = first + second - third
            for d in range(row_parts):
                span = slice(d * part_rows, (d + 1) * part_rows)
                out_refs[d][m, 0] = out_refs[d][m, 0] + real[span]
                out_refs[d][m, 1] = out_refs[d][m, 1] + imag[span]
            return carry

        lax.fori_loop(first_m, first_m + count, row_block, 0)

    def trailing_at(t, table_ref):
        code = jnp.maximum(table_ref[plan.col_code + t], 0)
        return (0, 0, 0, plan.own_col(code))

    out_shape = (row_cap, 2, part_rows, BLK)
    return pl.pallas_call(
        kernel,
        grid_spec=pltpu.PrefetchScalarGridSpec(
            num_scalar_prefetch=1,
            grid=(gathered[0].shape[0],),
            in_specs=[pl.BlockSpec((1, 2, piece, BLK), lambda t, table_ref: (t, 0, 0, 0)) for _ in range(members)]
            + [pl.BlockSpec((1, 2, trailing.shape[2], BLK), trailing_at)],
            out_specs=[
                pl.BlockSpec(out_shape, lambda t, table_ref: (0, 0, 0, 0))
                for _ in range(row_parts)
            ],
            scratch_shapes=[pltpu.VMEM((3, rows, 3 * BLK), jnp.bfloat16)],
        ),
        out_shape=[jax.ShapeDtypeStruct(out_shape, jnp.float32) for _ in range(row_parts)],
        name="partial_off",
    )(table, *gathered, trailing)


def weighted_corner(plan, table, weights, pivot, panels, offs):
    supers = plan.supers
    groups = len(panels[0])
    flat_panels = [panel for group in panels for panel in group]
    piece = flat_panels[0].shape[2]
    rows = groups * piece
    width = offs[0].shape[2]

    def kernel(table_ref, weights_ref, pivot_ref, *refs):
        panel_refs = refs[: len(flat_panels)]
        off_refs = refs[len(flat_panels) : len(flat_panels) + len(offs)]
        out_ref, left_ref, right_ref = refs[-3:]
        row = table_ref[plan.here]
        col = table_ref[plan.here + 1]
        out_ref[...] = jnp.zeros(out_ref.shape, jnp.float32)

        def pair(f, carry):
            part_row = table_ref[plan.part_of_row + f]

            @pl.when(part_row >= 0)
            def _():
                row_slot = jnp.bitwise_xor(part_row, col)
                m = table_ref[plan.rank_of_row + f]
                col_slot = jnp.bitwise_xor(table_ref[plan.part_of_col + f], row)
                t = table_ref[plan.rank_of_col + f]
                for d in range(len(offs)):

                    @pl.when(row_slot == d)
                    def _(d=d):
                        off_re = off_refs[d][m, 0]
                        off_im = off_refs[d][m, 1]
                        right_ref[0] = right_terms(off_re)
                        right_ref[1] = right_terms(off_im)
                        right_ref[2] = right_terms(off_re + off_im)

                for d in range(len(panels)):

                    @pl.when(col_slot == d)
                    def _(d=d):
                        for g in range(groups):
                            span = slice(g * piece, (g + 1) * piece)
                            left_re = panel_refs[d * groups + g][t, 0]
                            left_im = panel_refs[d * groups + g][t, 1]
                            left_ref[0, span, :] = left_terms(left_re)
                            left_ref[1, span, :] = left_terms(left_im)
                            left_ref[2, span, :] = left_terms(left_re + left_im)

                k = quotient(f, plan.slots)
                first = contract(left_ref[0], right_ref[0])
                second = contract(left_ref[1], right_ref[1])
                third = contract(left_ref[2], right_ref[2])
                out_ref[k, 0] = out_ref[k, 0] + (first - second)
                out_ref[k, 1] = out_ref[k, 1] + (third - first - second)

            return carry

        lax.fori_loop(0, plan.pairs, pair, 0)
        weight_re = weights_ref[0, 0]
        weight_im = weights_ref[0, 1]
        for k in range(supers):
            corner_re = pivot_ref[k, 0] - out_ref[k, 0]
            corner_im = pivot_ref[k, 1] - out_ref[k, 1]
            out_ref[k, 0] = weight_re * corner_re - weight_im * corner_im
            out_ref[k, 1] = weight_re * corner_im + weight_im * corner_re

    smem = pl.BlockSpec(memory_space=pltpu.SMEM)
    vmem = pl.BlockSpec(memory_space=pltpu.VMEM)
    return pl.pallas_call(
        kernel,
        in_specs=[smem, smem] + [vmem] * (1 + len(flat_panels) + len(offs)),
        out_specs=vmem,
        out_shape=jax.ShapeDtypeStruct((supers, 2, rows, width), jnp.float32),
        scratch_shapes=[
            pltpu.VMEM((3, rows, 3 * BLK), jnp.bfloat16),
            pltpu.VMEM((3, width, 3 * BLK), jnp.bfloat16),
        ],
        name="corner",
    )(table, weights, pivot, *flat_panels, *offs)


def spread(plan, table, offs, share):
    groups = len(offs)
    part_rows = offs[0].shape[2]
    piece = part_rows // share
    rows = groups * part_rows

    def kernel(table_ref, *refs):
        out_ref = refs[-1]
        slot = table_ref[plan.out_slot + pl.program_id(0) * plan.row_blocks + pl.program_id(1)]

        @pl.when(slot >= 0)
        def _():
            for g in range(groups):
                for s in range(share):
                    at = (s * groups + g) * piece
                    out_ref[0, 0, :, at : at + piece, :] = refs[g][
                        0, :, s * piece : (s + 1) * piece, :
                    ]

        @pl.when(slot < 0)
        def _():
            out_ref[...] = jnp.zeros(out_ref.shape, jnp.float32)

    def off_at(k, i, table_ref):
        slot = table_ref[plan.out_slot + k * plan.row_blocks + i]
        return (jnp.maximum(slot, 0), 0, 0, 0)

    return pl.pallas_call(
        kernel,
        grid_spec=pltpu.PrefetchScalarGridSpec(
            num_scalar_prefetch=1,
            grid=(plan.supers, plan.row_blocks),
            in_specs=[pl.BlockSpec((1, 2, part_rows, BLK), off_at) for _ in range(groups)],
            out_specs=pl.BlockSpec(
                (1, 1, 2, rows, BLK), lambda k, i, table_ref: (0, k, 0, 0, i)
            ),
        ),
        out_shape=jax.ShapeDtypeStruct(
            (1, plan.supers, 2, rows, plan.row_blocks * BLK), jnp.float32
        ),
        name="spread",
    )(table, *offs)


def after(value, *others):
    return lax.optimization_barrier((value, *others))[0]


def run(plan, caps, trailing, lower_panel, pivot_inverse, pole_weights, table):
    col_cap, row_cap = caps
    row_parts = lax.axis_size("row")
    col_parts = lax.axis_size("col")
    share = col_parts // row_parts
    packed = pack_columns(plan, table, lower_panel, col_cap, CHUNKS)
    piece = packed[0].shape[2]
    panels = [None] * CHUNKS
    panels[0] = gather_xor(packed[0], "row")
    kept = []
    gathered = None
    for g in range(CHUNKS):
        source = packed[g] if gathered is None else after(packed[g], gathered[-1])
        gathered = gather_xor(source, "col")
        kept.append(partial_off(plan, table, trailing, gathered, row_cap, row_parts))
    offs = []
    for g in range(CHUNKS):
        parts = kept[g]
        if offs:
            parts = [parts[0]] + [after(part, offs[-1]) for part in parts[1:]]
        for bit in bits_down(row_parts):
            parts = [parts[d] + swap(parts[d | bit], "row", bit) for d in range(bit)]
        offs.append(parts[0])
    for g in range(1, CHUNKS):
        panels[g] = gather_xor(after(packed[g], offs[-1]), "row")
    by_row = [[panels[g][d] for g in range(CHUNKS)] for d in range(row_parts)]
    tiles = []
    last = None
    for g in range(CHUNKS):
        source = offs[g] if last is None else after(offs[g], last)
        every = gather_xor(source, "col")
        last = every[-1]
        pivot = jnp.concatenate(
            [
                pivot_inverse[0, :, :, :, (s * CHUNKS + g) * piece : (s * CHUNKS + g + 1) * piece]
                for s in range(share)
            ],
            axis=3,
        )
        tile = weighted_corner(plan, table, pole_weights, pivot, by_row, every)
        for bit in (1 << at for at in range(int(math.log2(lax.axis_size("pole"))))):
            tile = tile + swap(tile, "pole", bit)
        tiles.append(tile)
    density = jnp.concatenate(
        [
            tiles[g][..., s * piece : (s + 1) * piece]
            for s in range(share)
            for g in range(CHUNKS)
        ],
        axis=3,
    )
    return spread(plan, table, offs, share), density


def body(trailing, lower_panel, pivot_inverse, pole_weights, listed, list_counts):
    row_parts = lax.axis_size("row")
    col_parts = lax.axis_size("col")
    rows_here, cols_here = trailing.shape[2:]
    plan = Plan(
        listed.shape[0],
        listed.shape[1],
        rows_here * col_parts // BLK,
        cols_here // BLK,
        rows_here // BLK,
    )
    table, fill_col, fill_row = plan.table(
        listed, list_counts, lax.axis_index("row"), lax.axis_index("col"), row_parts, col_parts
    )
    caps = []
    for col_part, row_part in zip(COL_FRACTIONS, ROW_FRACTIONS):
        cap = (math.ceil(plan.max_cols * col_part), math.ceil(plan.max_rows * row_part))
        if cap not in caps:
            caps.append(cap)
    level = jnp.int32(0)
    for col_cap, row_cap in caps[:-1]:
        level = level + ((fill_col > col_cap) | (fill_row > row_cap)).astype(jnp.int32)
    return lax.switch(
        level,
        [functools.partial(run, plan, cap) for cap in caps],
        trailing,
        lower_panel,
        pivot_inverse,
        pole_weights,
        table,
    )


def solution(mesh):
    in_specs = (
        P("pole", None, "col", "row"),
        P("pole", None, None, "col", "row"),
        P("pole", None, None, "col", "row"),
        P("pole", None),
        P(),
        P(),
    )
    out_specs = (P("pole", None, None, "row", "col"), P(None, None, "col", "row"))
    return jax.shard_map(body, mesh=mesh, in_specs=in_specs, out_specs=out_specs, check_vma=False)
```
